32 devices in a mesh: grp: 2 (over y), smp: 4 (over x, core), row: 4 (over z).
Axes of the slice: x: 2, y: 2, z: 4, core: 2. Of those that a mesh axis runs over, the one named last changes fastest.
Arguments:
- positions: float32 [8, 3, 4096], P(('grp', 'smp'), None, 'row'), parts along dimension 0, may hold values from -60 to 60
- noise_draw: float32 [8, 3, 4096], P(('grp', 'smp'), None, 'row'), parts along dimension 0, may hold values from -6 to 6
- noise_level: float32 [8], P(('grp', 'smp')), parts along dimension 0, may hold values from 0.5 to 80
- atom_single: bfloat16 [8192, 128], P(('grp', 'row')), parts along dimension 0, may hold values from -6 to 6
- token_single: bfloat16 [1024, 768], P(('grp', 'row')), parts along dimension 0, may hold values from -6 to 6
- pair_cond: bfloat16 [1024, 512, 128], P(('grp', 'row'), 'smp'), parts along dimension 0, may hold values from -6 to 6
- atom_to_token: int32 [8192], P(('grp', 'row')), parts along dimension 0, may hold values from 0 to 511, as said below
- window_offsets: int32 [256], P(('grp', 'row')), parts along dimension 0, may hold values from -96 to 0
- atom_mask: int32 [8192], P('grp'), parts along dimension 0, may hold values 0 or 1
- token_mask: int32 [1024], P('grp'), parts along dimension 0, may hold values 0 or 1
- coord_in: float32 [3, 128], replicated, may hold values from -3.5 to 3.5
- atom_gain: float32 [2, 128], replicated, may hold values from 0.1 to 1.9
- atom_qkv: bfloat16 [2, 128, 384], replicated, may hold values from -1 to 1
- atom_proj: bfloat16 [2, 128, 128], replicated, may hold values from -0.5 to 0.5
- gather_in: bfloat16 [128, 768], replicated, may hold values from -0.5 to 0.5
- noise_embed: float32 [768], replicated, may hold values from -6 to 6
- pair_gain: float32 [128], replicated, may hold values from 0.1 to 1.9
- pair_heads: bfloat16 [128, 16], replicated, may hold values from -0.5 to 0.5
- token_gain: float32 [2, 768], replicated, may hold values from 0.1 to 1.9
- token_qkv: bfloat16 [768, 2304], replicated, may hold values from -1 to 1
- token_proj: bfloat16 [768, 768], replicated, may hold values from -0.21875 to 0.21875
- ffn_in: bfloat16 [768, 3072], replicated, may hold values from -0.21875 to 0.21875
- ffn_out: bfloat16 [1536, 768], replicated, may hold values from -0.15625 to 0.15625
- scatter_out: bfloat16 [768, 128], replicated, may hold values from -0.21875 to 0.21875
- out_gain: float32 [128], replicated, may hold values from 0.1 to 1.9
- coord_out: bfloat16 [3, 128], replicated, may hold values from -0.5 to 0.5
Outputs:
- token_out: bfloat16 [8, 512, 768], P(('grp', 'smp'), 'row'), parts along dimension 0
- direction: float32 [8, 3, 4096], P(('grp', 'smp'), None, 'row'), parts along dimension 0
The draws below stay inside these ranges and needn't reach their ends.
There are 2 independent parts, one for each index of `grp`. The reference program is written for one: setup_inputs(seed, part) draws one part's arguments, and reference() takes and returns one part's arrays. A program takes and returns all parts, laid end to end along the dimension named above; an argument that names none is the same for every part. Nothing has to cross between parts.
Inputs may be any that keep to these rules, and one draw needn't show every extreme that they name: `atom_to_token`: never falls along the atoms; atoms k * 1024 to (k + 1) * 1024 - 1 belong to tokens k * 128 to (k + 1) * 128 - 1; some tokens have no atom.
All inputs are finite; a program needn't handle non-finite values.
Results may differ from the reference program's by a relative error of at most 0.013.
Values may be sent and summed in bfloat16 or wider, within the bound.
A program may use at most 128 MiB of HBM per device.

```python
import math
import jax
import jax.numpy as jnp
from jax import lax

D = 768
HEADS = 16
FF = 1536
CP = 128
CA = 128
AHEADS = 4
TOKR = 128
WQ = 32
WK = 128
HALO = 96
ATOMR = 1024
TOK = 512
ATOMS = 4096
SAMPLES = 4


def draw_atom_to_token(key, part):
    block_total = ATOMS // ATOMR
    local_ids = jax.random.randint(jax.random.fold_in(key, 11), (block_total, ATOMR), 0, TOKR)
    empty_ids = jax.random.randint(jax.random.fold_in(key, 12), (block_total, 2), 0, TOKR - 1)
    for column in range(2):
        local_ids = jnp.where(local_ids == empty_ids[:, column:column + 1], local_ids + 1, local_ids)
    local_ids = jnp.minimum(local_ids, TOKR - 1)
    local_ids = jnp.sort(local_ids, axis=1)
    local_ids = local_ids.at[:, 0].set(0).at[:, ATOMR - 1].set(TOKR - 1)
    base_ids = jnp.arange(block_total, dtype=jnp.int32)[:, None] * TOKR
    return (local_ids + base_ids).reshape(ATOMS).astype(jnp.int32)


def draw_window_offsets(key, part):
    block_total = ATOMS // ATOMR
    per_device = ATOMR // WQ
    offsets = jax.random.randint(jax.random.fold_in(key, 21), (block_total, per_device), 0 - HALO, 1)
    offsets = offsets.at[:, 0].set(0 - HALO).at[:, per_device - 1].set(0)
    return offsets.reshape(block_total * per_device).astype(jnp.int32)


def single_features(key, count, width):
    values = jnp.clip(jax.random.normal(jax.random.fold_in(key, 1), (count, width), jnp.float32), -6.0, 6.0)
    return values.astype(jnp.bfloat16)


def draw_token_single(key, part):
    return single_features(key, TOK, D)


def draw_atom_single(key, part):
    return single_features(key, ATOMS, CA)


def weight_values(key, shape, fan_in):
    values = jax.random.truncated_normal(jax.random.fold_in(key, 6), -4.0, 4.0, shape, jnp.float32)
    return values / math.sqrt(fan_in)


def draw_token_qkv(key, part):
    matrix = weight_values(key, (D, 3 * D), D)
    return matrix.astype(jnp.bfloat16)


def draw_atom_qkv(key, part):
    matrix = weight_values(key, (2, CA, 3 * CA), CA)
    return matrix.astype(jnp.bfloat16)


def with_ends(values, own_key, low, high):
    longest = values.shape.index(max(values.shape))
    spots = []
    for shift in (0, 1):
        where = [jax.random.randint(jax.random.fold_in(own_key, axis), (), 0, length) for axis, length in enumerate(values.shape)]
        where[longest] = (where[longest] + shift) % values.shape[longest]
        spots.append(tuple(where))
    return values.at[spots[0]].set(low).at[spots[1]].set(high)


def block_levels(stream_key, dims, shards, smallest, high):
    level, own = 1.0, jax.random.fold_in(stream_key, 6)
    for position, parts in shards:
        draws = jnp.exp(jax.random.uniform(jax.random.fold_in(own, position), (parts,), jnp.float32, smallest / len(shards), high / len(shards)))
        level = level * jnp.repeat(draws, dims[position] // parts).reshape([-1 if axis == position else 1 for axis in range(len(dims))])
    return level


def gaussian(stream_key, extent, spread, bound, split=(), held_as=jnp.bfloat16):
    level = block_levels(stream_key, extent, split, -0.22, 0.18) if split else 1.0
    result = jax.random.normal(stream_key, extent, jnp.float32) * spread * level
    return jnp.minimum(jnp.maximum(result, -bound), bound).astype(held_as)


def setup_inputs(seed: int = 0, part: int = 0) -> dict:
    arg_keys = jax.random.split(jax.random.key(seed), 27)
    part_splits = jax.random.split(jax.random.fold_in(arg_keys[26], part), 27)
    positions = gaussian(part_splits[0], (SAMPLES, 3, ATOMS), 10.0, 60.0, ((0, 4), (2, 4)), jnp.float32)
    noise_draw = gaussian(part_splits[1], (SAMPLES, 3, ATOMS), 1.0, 6.0, ((0, 4), (2, 4)), jnp.float32)
    noise_level = jnp.clip(jnp.exp(math.log(80.0) - 5.075174 * jax.random.uniform(part_splits[2], (SAMPLES,), jnp.float32) ** block_levels(part_splits[2], (SAMPLES,), ((0, 4),), -0.2, 0.2)), 0.5, 80.0)
    atom_single = draw_atom_single(jax.random.fold_in(jax.random.fold_in(arg_keys[26], part), 71), part)
    token_single = draw_token_single(jax.random.fold_in(jax.random.fold_in(arg_keys[26], part), 71), part)
    pair_cond = gaussian(part_splits[5], (TOK, TOK, CP), 1.0, 6.0, ((0, 4), (1, 4)))
    atom_to_token = draw_atom_to_token(jax.random.fold_in(jax.random.fold_in(arg_keys[26], part), 71), part)
    window_offsets = draw_window_offsets(jax.random.fold_in(jax.random.fold_in(arg_keys[26], part), 71), part)
    atom_mask = with_ends((jax.random.randint(part_splits[8], (ATOMS,), 0, 8) < 7).astype(jnp.int32), jax.random.fold_in(part_splits[8], 1), 0, 1)
    token_mask = with_ends((jax.random.randint(part_splits[9], (TOK,), 0, 16) < 15).astype(jnp.int32), jax.random.fold_in(part_splits[9], 1), 0, 1)
    coord_in = gaussian(arg_keys[10], (3, CA), 3 ** -0.5, 3.5, (), jnp.float32)
    atom_gain = jnp.clip(1.0 + 0.18 * jax.random.normal(arg_keys[11], (2, CA), jnp.float32), 0.1, 1.9)
    atom_qkv = draw_atom_qkv(jax.random.fold_in(arg_keys[26], 71), part)
    atom_proj = gaussian(arg_keys[13], (2, CA, CA), CA ** -0.5, 0.5)
    gather_in = gaussian(arg_keys[14], (CA, D), CA ** -0.5, 0.5)
    noise_embed = gaussian(arg_keys[15], (D,), 1.0, 6.0, (), jnp.float32)
    pair_gain = jnp.clip(1.0 + 0.18 * jax.random.normal(arg_keys[16], (CP,), jnp.float32), 0.1, 1.9)
    pair_heads = gaussian(arg_keys[17], (CP, HEADS), CP ** -0.5, 0.5)
    token_gain = jnp.clip(1.0 + 0.18 * jax.random.normal(arg_keys[18], (2, D), jnp.float32), 0.1, 1.9)
    token_qkv = draw_token_qkv(jax.random.fold_in(arg_keys[26], 71), part)
    token_proj = gaussian(arg_keys[20], (D, D), D ** -0.5, 0.21875)
    ffn_in = gaussian(arg_keys[21], (D, 2 * FF), D ** -0.5, 0.21875)
    ffn_out = gaussian(arg_keys[22], (FF, D), FF ** -0.5, 0.15625)
    scatter_out = gaussian(arg_keys[23], (D, CA), D ** -0.5, 0.21875)
    out_gain = jnp.clip(1.0 + 0.18 * jax.random.normal(arg_keys[24], (CA,), jnp.float32), 0.1, 1.9)
    coord_out = gaussian(arg_keys[25], (3, CA), CA ** -0.5, 0.5)
    return dict(positions=positions, noise_draw=noise_draw, noise_level=noise_level, atom_single=atom_single, token_single=token_single, pair_cond=pair_cond, atom_to_token=atom_to_token, window_offsets=window_offsets, atom_mask=atom_mask, token_mask=token_mask, coord_in=coord_in, atom_gain=atom_gain, atom_qkv=atom_qkv, atom_proj=atom_proj, gather_in=gather_in, noise_embed=noise_embed, pair_gain=pair_gain, pair_heads=pair_heads, token_gain=token_gain, token_qkv=token_qkv, token_proj=token_proj, ffn_in=ffn_in, ffn_out=ffn_out, scatter_out=scatter_out, out_gain=out_gain, coord_out=coord_out)


sigma_data = 16.0
gamma_boost = 0.8
norm_eps = 1e-05
masked_score = -1e+30

def layer_norm(values, norm_gain):
    average = lax.optimization_barrier(jnp.mean(values, axis=-1, keepdims=True))
    centred = values - average
    variance = lax.optimization_barrier(jnp.mean(centred * centred, axis=-1, keepdims=True))
    return centred * lax.rsqrt(variance + norm_eps) * norm_gain

def softmax_rows(scores):
    largest = lax.optimization_barrier(jnp.max(scores, axis=-1, keepdims=True))
    exponent = jnp.exp(scores - largest)
    return exponent / lax.optimization_barrier(jnp.sum(exponent, axis=-1, keepdims=True))

def pair_bias_of(pair_tile, pair_gain, pair_heads):
    normed = layer_norm(pair_tile.astype(jnp.float32), pair_gain).astype(jnp.bfloat16)
    normed = lax.optimization_barrier(normed)
    return jnp.einsum('ijc,ch->hij', normed.astype(jnp.float32), pair_heads.astype(jnp.float32)).astype(jnp.bfloat16)

def window_attend(queries, windows, live, w_out):
    block_count = queries.shape[0] // WQ
    head_size = CA // AHEADS
    query_heads = queries.reshape(block_count, WQ, AHEADS, head_size).astype(jnp.float32)
    key_heads = windows[:, :, :CA].reshape(block_count, WK, AHEADS, head_size).astype(jnp.float32)
    value_heads = windows[:, :, CA:].reshape(block_count, WK, AHEADS, head_size).astype(jnp.float32)
    scores = jnp.einsum('bqhd,bkhd->bhqk', query_heads, key_heads) / jnp.sqrt(jnp.float32(head_size))
    scores = jnp.where(live[:, None, None, :], scores, masked_score)
    weights = lax.optimization_barrier(softmax_rows(scores).astype(jnp.bfloat16)).astype(jnp.float32)
    mixed_heads = jnp.einsum('bhqk,bkhd->bqhd', weights, value_heads).astype(jnp.bfloat16)
    return jnp.dot(mixed_heads.reshape(block_count * WQ, CA), w_out, preferred_element_type=jnp.float32)

def atom_block(atom_state, norm_gain, w_qkv, w_out, offsets, valid):
    atom_count = atom_state.shape[0]
    block_count = atom_count // WQ
    normed = layer_norm(atom_state, norm_gain).astype(jnp.bfloat16)
    projected = jnp.dot(normed, w_qkv, preferred_element_type=jnp.float32).astype(jnp.bfloat16)
    padded = jnp.pad(projected[:, CA:], ((HALO, HALO), (0, 0)))
    live_padded = jnp.pad(valid, (HALO, HALO))
    starts = jnp.arange(block_count, dtype=jnp.int32) * WQ + offsets + HALO
    window_index = starts[:, None] + jnp.arange(WK, dtype=jnp.int32)[None, :]
    return atom_state + window_attend(projected[:, :CA], padded[window_index], live_padded[window_index] > 0, w_out)

def reference(positions, noise_draw, noise_level, atom_single, token_single, pair_cond, atom_to_token, window_offsets, atom_mask, token_mask, coord_in, atom_gain, atom_qkv, atom_proj, gather_in, noise_embed, pair_gain, pair_heads, token_gain, token_qkv, token_proj, ffn_in, ffn_out, scatter_out, out_gain, coord_out):
    biases = pair_bias_of(pair_cond, pair_gain, pair_heads).astype(jnp.float32)
    token_ids = jnp.arange(TOK, dtype=jnp.int32)
    member = (atom_to_token[None, :] == token_ids[:, None]) & (atom_mask[None, :] > 0)
    onehot = member.astype(jnp.bfloat16)
    counts = jnp.maximum(lax.optimization_barrier(jnp.sum(member.astype(jnp.float32), axis=1)), 1.0)
    key_live = token_mask > 0
    head_size = D // HEADS

    def one_sample(sample_inputs):
        coords, kicks, level_now = sample_inputs
        level_hat = (1.0 + gamma_boost) * level_now
        noisy = coords + jnp.sqrt(level_hat * level_hat - level_now * level_now) * kicks
        scaled = noisy / jnp.sqrt(level_hat * level_hat + sigma_data * sigma_data)
        atom_state = atom_single.astype(jnp.float32) + jnp.einsum('ka,kc->ac', scaled, coord_in, precision=lax.Precision.HIGHEST)
        atom_state = atom_block(atom_state, atom_gain[0], atom_qkv[0], atom_proj[0], window_offsets, atom_mask)
        lifted = jax.nn.relu(jnp.dot(atom_state.astype(jnp.bfloat16), gather_in, preferred_element_type=jnp.float32)).astype(jnp.bfloat16)
        pooled = jnp.dot(onehot, lifted, preferred_element_type=jnp.float32) / counts[:, None]
        token_state = pooled + token_single.astype(jnp.float32) + jnp.log(level_hat / sigma_data) / 4.0 * noise_embed
        normed = layer_norm(token_state, token_gain[0]).astype(jnp.bfloat16)
        projected = jnp.dot(normed, token_qkv, preferred_element_type=jnp.float32).astype(jnp.bfloat16)
        query_heads = projected[:, :D].reshape(TOK, HEADS, head_size).astype(jnp.float32)
        key_heads = projected[:, D:2 * D].reshape(TOK, HEADS, head_size).astype(jnp.float32)
        value_heads = projected[:, 2 * D:].reshape(TOK, HEADS, head_size).astype(jnp.float32)
        scores = jnp.einsum('ihd,jhd->hij', query_heads, key_heads) / jnp.sqrt(jnp.float32(head_size)) + biases
        scores = jnp.where(key_live[None, None, :], scores, masked_score)
        weights = lax.optimization_barrier(softmax_rows(scores).astype(jnp.bfloat16)).astype(jnp.float32)
        mixed_heads = jnp.einsum('hij,jhd->ihd', weights, value_heads).astype(jnp.bfloat16).reshape(TOK, D)
        token_state = token_state + jnp.dot(mixed_heads, token_proj, preferred_element_type=jnp.float32)
        normed = layer_norm(token_state, token_gain[1]).astype(jnp.bfloat16)
        hidden = jnp.dot(normed, ffn_in, preferred_element_type=jnp.float32)
        active = (jax.nn.silu(hidden[:, :FF]) * hidden[:, FF:]).astype(jnp.bfloat16)
        token_state = token_state + jnp.dot(active, ffn_out, preferred_element_type=jnp.float32)
        token_result = token_state.astype(jnp.bfloat16)
        spread_back = jnp.dot(token_result, scatter_out, preferred_element_type=jnp.float32).astype(jnp.bfloat16)
        atom_state = atom_state + lax.dot_general(onehot, spread_back, (((0,), (0,)), ((), ())), preferred_element_type=jnp.float32)
        atom_state = atom_block(atom_state, atom_gain[1], atom_qkv[1], atom_proj[1], window_offsets, atom_mask)
        normed_out = layer_norm(atom_state, out_gain).astype(jnp.bfloat16)
        update = lax.dot_general(coord_out, normed_out, (((1,), (1,)), ((), ())), preferred_element_type=jnp.float32)
        base_square = sigma_data * sigma_data + level_hat * level_hat
        skip_scale = sigma_data * sigma_data / base_square
        out_scale = level_hat * sigma_data / jnp.sqrt(base_square)
        denoised = skip_scale * noisy + out_scale * update
        return (token_result, (noisy - denoised) / level_hat)
    token_out, direction = lax.map(one_sample, (positions, noise_draw, noise_level))
    return (token_out, direction)
```

```python
import functools
import jax
import jax.numpy as jnp
from jax import lax
from jax.experimental import pallas as pl
from jax.experimental.pallas import tpu as pltpu
from jax.sharding import PartitionSpec as P

HEADS = 16
AHEADS = 4
WQ = 32
WK = 128
HALO = 96
GQ = 64
HALVES = 2

sigma_data = 16.0
gamma_boost = 0.8
norm_eps = 1e-05
masked_score = -1e30
outside_score = -2e30

f32 = jnp.float32
bf16 = jnp.bfloat16
MESH = pl.DeviceIdType.MESH


def mm(a, b):
    return jnp.dot(a, b, preferred_element_type=f32)


def mm_nt(a, b):
    return lax.dot_general(a, b, (((1,), (1,)), ((), ())), preferred_element_type=f32)


def mm_tn(a, b):
    return lax.dot_general(a, b, (((0,), (0,)), ((), ())), preferred_element_type=f32)


def layer_norm(values, norm_gain):
    average = jnp.mean(values, axis=-1, keepdims=True)
    centred = values - average
    variance = jnp.mean(centred * centred, axis=-1, keepdims=True)
    return centred * lax.rsqrt(variance + norm_eps) * norm_gain


def lanes(shape):
    return lax.broadcasted_iota(jnp.int32, shape, len(shape) - 1)


def kernel(
    n_row, n_smp,
    positions, noise_draw, noise_level, atom_single, token_single, pair_cond,
    atom_to_token, window_offsets, atom_mask, token_mask, coord_in, atom_gain, atom_qkv,
    atom_proj, gather_in, noise_embed, pair_gain, pair_heads, token_gain, token_qkv,
    token_proj, ffn_in, ffn_out, scatter_out, out_gain, coord_out,
    token_out, direction,
    pair_v, qkv_v, proj_v, fin_v, fout_v,
    spread_heads, bias_all, next_all, q_atom, kv_atom, halo_n, halo_o, mixed_atom, state,
    tokens_all, k_all, v_all, q_tok, mixed_tok, token_state, mask_rows,
    w_sem, pair_sem, halo_send, halo_recv, tok_right, tok_left, tok_recv,
    bias_sx, bias_sib, bias_recv,
):
    row = lax.axis_index("row")
    smp = lax.axis_index("smp")
    cores = 2 if n_smp % 2 == 0 else 1
    n_x = n_smp // cores
    my_x, my_c = smp // cores, smp % cores
    atom_rows, ca = atom_single.shape
    tok_rows, d_model = token_single.shape
    ff = fout_v.shape[0]
    key_count = tok_rows * n_row
    j_keys = pair_cond.shape[1]
    half_rows = tok_rows // HALVES
    head_size = d_model // HEADS
    mask_tiles = atom_rows // 128

    loads = [
        pltpu.make_async_copy(token_qkv, qkv_v, w_sem.at[0]),
        pltpu.make_async_copy(token_proj, proj_v, w_sem.at[1]),
        pltpu.make_async_copy(ffn_in, fin_v, w_sem.at[2]),
        pltpu.make_async_copy(ffn_out, fout_v, w_sem.at[3]),
    ]
    pair_loads = [
        pltpu.make_async_copy(
            pair_cond.at[pl.ds(half * half_rows, half_rows)],
            pair_v.at[pl.ds(half * half_rows, half_rows)],
            pair_sem.at[half],
        )
        for half in range(HALVES)
    ]
    pair_loads[0].start()
    pair_loads[1].start()
    for load in loads:
        load.start()

    barrier = pltpu.get_barrier_semaphore()
    smp_peers = [((my_x + d) % n_x) * cores + my_c for d in range(1, n_x)]
    if cores == 2:
        smp_peers.append(my_x * cores + (1 - my_c))
    for peer in smp_peers:
        pl.semaphore_signal(barrier, inc=1, device_id={"smp": peer}, device_id_type=MESH)

    @pl.when(row > 0)
    def _():
        pl.semaphore_signal(barrier, inc=1, device_id={"row": row - 1}, device_id_type=MESH)

    @pl.when(row < n_row - 1)
    def _():
        pl.semaphore_signal(barrier, inc=1, device_id={"row": row + 1}, device_id_type=MESH)

    has_left = (row + n_row - 1) // n_row
    has_right = (2 * n_row - 2 - row) // n_row


    def halo_copies(phase):
        right = pltpu.make_async_remote_copy(
            src_ref=next_all.at[phase, pl.ds(atom_rows - HALO, HALO)],
            dst_ref=halo_n.at[phase, 0],
            send_sem=halo_send.at[phase, 0],
            recv_sem=halo_recv.at[phase, 0],
            device_id={"row": row + 1},
            device_id_type=MESH,
        )
        left = pltpu.make_async_remote_copy(
            src_ref=next_all.at[phase, pl.ds(0, HALO)],
            dst_ref=halo_n.at[phase, 1],
            send_sem=halo_send.at[phase, 1],
            recv_sem=halo_recv.at[phase, 1],
            device_id={"row": row - 1},
            device_id_type=MESH,
        )
        return right, left

    def halo_start(phase):
        right, left = halo_copies(phase)

        @pl.when(row < n_row - 1)
        def _():
            right.start()

        @pl.when(row > 0)
        def _():
            left.start()

    def halo_finish(phase, w_kv):
        right, left = halo_copies(phase)
        for side, here, copy, base in (
            (0, row > 0, right, 0),
            (1, row < n_row - 1, left, HALO + atom_rows),
        ):

            @pl.when(here)
            def _():
                copy.wait_recv()
                kv_atom[pl.ds(base, HALO), :] = mm(halo_n[phase, side], w_kv).astype(bf16)

            @pl.when(jnp.logical_not(here))
            def _():
                kv_atom[pl.ds(base, HALO), :] = jnp.zeros((HALO, 2 * ca), bf16)

        @pl.when(row < n_row - 1)
        def _():
            right.wait_send()

        @pl.when(row > 0)
        def _():
            left.wait_send()

    level = noise_level[...]
    level_hat = (1.0 + gamma_boost) * level
    noisy = positions[...] + jnp.sqrt(level_hat * level_hat - level * level) * noise_draw[...]
    scaled = noisy / jnp.sqrt(level_hat * level_hat + sigma_data * sigma_data)
    state[...] = atom_single[...].astype(f32) + lax.dot_general(
        scaled, coord_in[...], (((0,), (0,)), ((), ())),
        precision=lax.Precision.HIGHEST, preferred_element_type=f32,
    )

    def mask_row(tile):
        top = n_row * mask_tiles
        inside = jnp.logical_and(tile >= 0, tile < top)
        safe = jnp.clip(tile, 0, top - 1)
        values = atom_mask[pl.ds(safe, 1), :].astype(f32)
        return jnp.where(inside, values, jnp.zeros_like(values))

    def build_masks(pair, carry):
        tile = row * mask_tiles + pair
        wide = jnp.concatenate(
            [mask_row(tile - 1), mask_row(tile), mask_row(tile + 1), jnp.zeros((1, 128), f32)], axis=1
        )
        wide = jnp.broadcast_to(wide, (8, 512))
        for odd in range(2):
            start = 32 + 64 * odd
            moved = pltpu.roll(wide, 512 - start, 1)
            mask_rows[2 * pair + odd] = moved[:, :256]
        return carry

    lax.fori_loop(0, mask_tiles, build_masks, 0)

    def normalise_and_send(phase):
        next_all[phase] = layer_norm(state[...], atom_gain[pl.ds(phase, 1), :]).astype(bf16)

    normalise_and_send(0)
    pl.semaphore_wait(barrier, len(smp_peers) + has_left + has_right)
    halo_start(0)

    unit = 8
    for i in range(unit):
        pick = lanes((HEADS, 128)) == (
            lax.broadcasted_iota(jnp.int32, (HEADS, 128), 0) * unit + i
        )
        spread_heads[pl.ds(i * 128, 128), :] = mm(
            pair_heads[...], pick.astype(f32).astype(bf16)
        ).astype(bf16)
    mean_matrix = jnp.full((ca, ca), 1.0 / ca, bf16)

    def bias_half(half):
        pair_loads[half].wait()

        def body(step, carry):
            base = half * half_rows + step * 16
            parts = []
            for sub in range(2):
                total = None
                for i in range(unit):
                    x = pair_v[base + sub * unit + i]
                    centred = x.astype(f32) - mm(x, mean_matrix)
                    variance = mm((centred * centred).astype(bf16), mean_matrix)
                    normed = (centred * lax.rsqrt(variance + norm_eps) * pair_gain[...]).astype(bf16)
                    term = mm(normed, spread_heads[pl.ds(i * 128, 128), :])
                    total = term if total is None else total + term
                parts.append(jnp.transpose(total).reshape(HEADS, unit, j_keys))
            both = jnp.concatenate(parts, axis=1).astype(bf16)
            bias_all[smp, half, :, pl.ds(pl.multiple_of(step * 16, 16), 16), :] = both
            return carry

        lax.fori_loop(0, half_rows // 16, body, 0)

    def bias_x(half, d):
        return pltpu.make_async_remote_copy(
            src_ref=bias_all.at[smp, half],
            dst_ref=bias_all.at[smp, half],
            send_sem=bias_sx.at[half, d],
            recv_sem=bias_recv.at[half, smp],
            device_id={"smp": ((my_x + d) % n_x) * cores + my_c},
            device_id_type=MESH,
        )

    def bias_to_sibling(half, d):
        slot = ((my_x + n_x - d) % n_x) * cores + my_c
        return pltpu.make_async_remote_copy(
            src_ref=bias_all.at[slot, half],
            dst_ref=bias_all.at[slot, half],
            send_sem=bias_sib.at[half, d],
            recv_sem=bias_recv.at[half, slot],
            device_id={"smp": my_x * cores + (1 - my_c)},
            device_id_type=MESH,
        )

    def bias_arrival(half, d, core):
        slot = ((my_x + n_x - d) % n_x) * cores + core
        return pltpu.make_async_remote_copy(
            src_ref=bias_all.at[slot, half],
            dst_ref=bias_all.at[slot, half],
            send_sem=bias_sx.at[half, 0],
            recv_sem=bias_recv.at[half, slot],
            device_id={"smp": my_x * cores + (1 - my_c) if cores == 2 else smp},
            device_id_type=MESH,
        )

    def bias_send(half):
        for d in range(1, n_x):
            bias_x(half, d).start()
        if cores == 2:
            bias_to_sibling(half, 0).start()

    def bias_relay(half):
        for d in range(1, n_x):
            bias_arrival(half, d, my_c).wait_recv()
            if cores == 2:
                bias_to_sibling(half, d).start()

    def bias_finish(half):
        for d in range(n_x):
            if cores == 2:
                bias_arrival(half, d, 1 - my_c).wait_recv()
                bias_to_sibling(half, d).wait_send()
            if d:
                bias_x(half, d).wait_send()

    head_of_lane = lanes((GQ, ca)) // (ca // AHEADS)
    atom_scale = 1.0 / float(ca // AHEADS) ** 0.5
    group_count = atom_rows // GQ

    def attend_group(group):
        start = pl.multiple_of(group * GQ, GQ)
        queries = q_atom[pl.ds(start, GQ), :]
        zero = jnp.zeros_like(queries)
        stacked = jnp.concatenate(
            [jnp.where(head_of_lane == h, queries, zero) for h in range(AHEADS)], axis=0
        )
        keys = kv_atom[pl.ds(start, 256), :ca]
        values = kv_atom[pl.ds(start, 256), ca:]
        scores = mm_nt(stacked, keys) * atom_scale
        dead = jnp.where(mask_rows[group] > 0, 0.0, masked_score)
        relative = lanes((8, 256))
        rows = []
        for u in range(GQ // WQ):
            first = window_offsets[group * (GQ // WQ) + u] + (HALO + WQ * u)
            inside = (relative >= first) & (relative < first + WK)
            own = jnp.where(inside, dead, outside_score)
            rows += [own] * (WQ // 8)
        limits = jnp.concatenate(rows, axis=0)
        scores = scores.reshape(AHEADS, GQ, 256) + limits[None]
        scores = scores.reshape(AHEADS * GQ, 256)
        largest = jnp.max(scores, axis=-1, keepdims=True)
        exponent = jnp.exp(scores - largest)
        total = jnp.sum(exponent, axis=-1, keepdims=True)
        mixed = mm(exponent.astype(bf16), values) / total
        result = jnp.zeros((GQ, ca), f32)
        for h in range(AHEADS):
            result = jnp.where(head_of_lane == h, mixed[h * GQ : (h + 1) * GQ], result)
        mixed_atom[pl.ds(start, GQ), :] = result.astype(bf16)

    def atom_block(phase, between):
        w_qkv = atom_qkv[phase]
        projected = mm(next_all[phase], w_qkv).astype(bf16)
        q_atom[...] = projected[:, :ca]
        kv_atom[pl.ds(HALO, atom_rows), :] = projected[:, ca:]
        between()

        def body(group, carry):
            attend_group(group)
            return carry

        lax.fori_loop(2, group_count - 2, body, 0, unroll=2)
        halo_finish(phase, w_qkv[:, ca:])

        def edge(k, carry):
            attend_group(k + (k // 2) * (group_count - 4))
            return carry

        lax.fori_loop(0, 4, edge, 0, unroll=2)
        state[...] = state[...] + mm(mixed_atom[...], atom_proj[phase])

    def first_half():
        bias_half(0)
        bias_send(0)

    atom_block(0, first_half)

    ids = atom_to_token[...] - row * tok_rows
    valid = jnp.concatenate([mask_row(row * mask_tiles + k) for k in range(mask_tiles)], axis=1)
    member = (lax.broadcasted_iota(jnp.int32, (tok_rows, atom_rows), 0) == ids) & (valid > 0)
    onehot32 = member.astype(f32)
    onehot = onehot32.astype(bf16)
    counts = jnp.maximum(jnp.sum(onehot32, axis=1, keepdims=True), 1.0)
    lifted = jnp.maximum(mm(state[...].astype(bf16), gather_in[...]), 0.0).astype(bf16)
    token_state[...] = (
        mm(onehot, lifted) / counts
        + token_single[...].astype(f32)
        + jnp.log(level_hat / sigma_data) / 4.0 * noise_embed[...]
    )
    tokens_all[row] = layer_norm(token_state[...], token_gain[0:1, :]).astype(bf16)

    def token_copy(slot, sem, target):
        return pltpu.make_async_remote_copy(
            src_ref=tokens_all.at[slot],
            dst_ref=tokens_all.at[slot],
            send_sem=sem.at[slot],
            recv_sem=tok_recv.at[slot],
            device_id={"row": target},
            device_id_type=MESH,
        )

    @pl.when(row < n_row - 1)
    def _():
        token_copy(row, tok_right, row + 1).start()

    @pl.when(row > 0)
    def _():
        token_copy(row, tok_left, row - 1).start()

    bias_half(1)
    bias_send(1)
    bias_relay(0)

    def project_keys(slot):
        x = tokens_all[slot]
        base = pl.multiple_of(slot * tok_rows, tok_rows)
        k_all[pl.ds(base, tok_rows), :] = mm(x, qkv_v[:, d_model : 2 * d_model]).astype(bf16)
        v_all[pl.ds(base, tok_rows), :] = mm(x, qkv_v[:, 2 * d_model :]).astype(bf16)

    loads[0].wait()
    q_tok[...] = mm(tokens_all[row], qkv_v[:, :d_model]).astype(bf16)
    project_keys(row)
    for t in range(1, n_row):

        @pl.when(row >= t)
        def _():
            slot = row - t
            token_copy(slot, tok_left, row - 1).wait_recv()

            @pl.when(row < n_row - 1)
            def _():
                token_copy(slot, tok_right, row + 1).start()

        @pl.when(row + t < n_row)
        def _():
            slot = row + t
            token_copy(slot, tok_right, row + 1).wait_recv()

            @pl.when(row > 0)
            def _():
                token_copy(slot, tok_left, row - 1).start()

        if t == n_row // 2:
            bias_relay(1)

        @pl.when(row >= t)
        def _():
            project_keys(row - t)

        @pl.when(row + t < n_row)
        def _():
            project_keys(row + t)

    bias_finish(0)
    bias_finish(1)

    mixed_tok[...] = jnp.zeros_like(mixed_tok)
    dead_keys = jnp.where(token_mask[...] > 0, 0.0, masked_score)
    token_scale = 1.0 / float(head_size) ** 0.5
    for h in range(HEADS):
        low = min(h * head_size // 128, d_model // 128 - 2) * 128
        window = lanes((tok_rows, 256)) + low
        mine = (window >= h * head_size) & (window < (h + 1) * head_size)
        queries = q_tok[:, low : low + 256]
        queries = jnp.where(mine, queries, jnp.zeros_like(queries))
        bias = jnp.concatenate(
            [bias_all[s, :, h].reshape(tok_rows, j_keys).astype(f32) for s in range(n_smp)], axis=1
        )
        scores = mm_nt(queries, k_all[:, low : low + 256]) * token_scale + bias + dead_keys
        largest = jnp.max(scores, axis=-1, keepdims=True)
        exponent = jnp.exp(scores - largest)
        total = jnp.sum(exponent, axis=-1, keepdims=True)
        mixed = mm(exponent.astype(bf16), v_all[:, low : low + 256]) / total
        mixed_tok[:, low : low + 256] = jnp.where(mine, mixed, mixed_tok[:, low : low + 256])

    loads[1].wait()
    token_state[...] = token_state[...] + mm(mixed_tok[...].astype(bf16), proj_v[...])
    normed = layer_norm(token_state[...], token_gain[1:2, :]).astype(bf16)
    loads[2].wait()
    gate = mm(normed, fin_v[:, :ff])
    active = (gate / (1.0 + jnp.exp(-gate)) * mm(normed, fin_v[:, ff:])).astype(bf16)
    loads[3].wait()
    result = (token_state[...] + mm(active, fout_v[...])).astype(bf16)
    token_out[...] = result
    spread_back = mm(result, scatter_out[...]).astype(bf16)
    state[...] = state[...] + mm_tn(onehot, spread_back)

    normalise_and_send(1)
    halo_start(1)
    atom_block(1, lambda: None)

    normed_out = layer_norm(state[...], out_gain[...]).astype(bf16)
    update = mm_nt(coord_out[...], normed_out)
    base_square = sigma_data * sigma_data + level_hat * level_hat
    skip_scale = sigma_data * sigma_data / base_square
    out_scale = level_hat * sigma_data / jnp.sqrt(base_square)
    denoised = skip_scale * noisy + out_scale * update
    direction[...] = (noisy - denoised) / level_hat

    for slot in range(n_row):

        @pl.when(jnp.logical_and(row < n_row - 1, slot <= row))
        def _():
            token_copy(slot, tok_right, row + 1).wait_send()

        @pl.when(jnp.logical_and(row > 0, slot >= row))
        def _():
            token_copy(slot, tok_left, row - 1).wait_send()


def per_device(n_row, n_smp, *args):
    (
        positions, noise_draw, noise_level, atom_single, token_single, pair_cond,
        atom_to_token, window_offsets, atom_mask, token_mask, coord_in, atom_gain, atom_qkv,
        atom_proj, gather_in, noise_embed, pair_gain, pair_heads, token_gain, token_qkv,
        token_proj, ffn_in, ffn_out, scatter_out, out_gain, coord_out,
    ) = args
    atom_rows, ca = atom_single.shape
    tok_rows, d_model = token_single.shape
    j_keys = pair_cond.shape[1]
    key_count = tok_rows * n_row
    vmem = pl.BlockSpec(memory_space=pltpu.VMEM)
    smem = pl.BlockSpec(memory_space=pltpu.SMEM)
    hbm = pl.BlockSpec(memory_space=pl.ANY)
    operands = (
        positions[0], noise_draw[0], noise_level.reshape(1, 1), atom_single, token_single,
        pair_cond, atom_to_token.reshape(1, -1), window_offsets, atom_mask.reshape(-1, 128),
        token_mask.reshape(1, -1), coord_in, atom_gain, atom_qkv, atom_proj, gather_in,
        noise_embed.reshape(1, -1), pair_gain.reshape(1, -1), pair_heads, token_gain, token_qkv,
        token_proj, ffn_in, ffn_out, scatter_out, out_gain.reshape(1, -1), coord_out,
    )
    specs = [vmem] * len(operands)
    specs[5] = hbm
    specs[7] = smem
    for i in (19, 20, 21, 22):
        specs[i] = hbm
    dma = pltpu.SemaphoreType.DMA
    token_out, direction = pl.pallas_call(
        functools.partial(kernel, n_row, n_smp),
        out_shape=(
            jax.ShapeDtypeStruct((tok_rows, d_model), bf16),
            jax.ShapeDtypeStruct(positions.shape[1:], f32),
        ),
        in_specs=specs,
        out_specs=(vmem, vmem),
        scratch_shapes=[
            pltpu.VMEM(pair_cond.shape, bf16),
            pltpu.VMEM(token_qkv.shape, bf16),
            pltpu.VMEM(token_proj.shape, bf16),
            pltpu.VMEM(ffn_in.shape, bf16),
            pltpu.VMEM(ffn_out.shape, bf16),
            pltpu.VMEM((8 * 128, 128), bf16),
            pltpu.VMEM((n_smp, HALVES, HEADS, tok_rows // HALVES, j_keys), bf16),
            pltpu.VMEM((2, atom_rows, ca), bf16),
            pltpu.VMEM((atom_rows, ca), bf16),
            pltpu.VMEM((atom_rows + 2 * HALO, 2 * ca), bf16),
            pltpu.VMEM((2, 2, HALO, ca), bf16),
            pltpu.VMEM((8, 128), bf16),
            pltpu.VMEM((atom_rows, ca), bf16),
            pltpu.VMEM((atom_rows, ca), f32),
            pltpu.VMEM((n_row, tok_rows, d_model), bf16),
            pltpu.VMEM((key_count, d_model), bf16),
            pltpu.VMEM((key_count, d_model), bf16),
            pltpu.VMEM((tok_rows, d_model), bf16),
            pltpu.VMEM((tok_rows, d_model), f32),
            pltpu.VMEM((tok_rows, d_model), f32),
            pltpu.VMEM((atom_rows // GQ, 8, 256), f32),
            dma((4,)),
            dma((HALVES,)),
            dma((2, 2)),
            dma((2, 2)),
            dma((n_row,)),
            dma((n_row,)),
            dma((n_row,)),
            dma((HALVES, n_smp)),
            dma((HALVES, n_smp)),
            dma((HALVES, n_smp)),
        ],
        compiler_params=pltpu.CompilerParams(
            collective_id=0, has_side_effects=True, vmem_limit_bytes=60 * 1024 * 1024
        ),
    )(*operands)
    return token_out[None], direction[None]


def solution(mesh):
    in_specs = (
        P(("grp", "smp"), None, "row"),
        P(("grp", "smp"), None, "row"),
        P(("grp", "smp")),
        P(("grp", "row"), None),
        P(("grp", "row"), None),
        P(("grp", "row"), "smp", None),
        P(("grp", "row")),
        P(("grp", "row")),
        P("grp"),
        P("grp"),
    ) + (P(),) * 16
    out_specs = (P(("grp", "smp"), "row", None), P(("grp", "smp"), None, "row"))
    return jax.shard_map(
        functools.partial(per_device, mesh.shape["row"], mesh.shape["smp"]),
        mesh=mesh, in_specs=in_specs, out_specs=out_specs, check_vma=False,
    )
```

```python
import functools
import jax
import jax.numpy as jnp
from jax import lax
from jax.experimental import pallas as pl
from jax.experimental.pallas import tpu as pltpu
from jax.sharding import PartitionSpec as P

HEADS = 16
AHEADS = 4
WQ = 32
WK = 128
HALO = 96
GQ = 64
HALVES = 2

sigma_data = 16.0
gamma_boost = 0.8
norm_eps = 1e-05
masked_score = -1e30
outside_score = -2e30

f32 = jnp.float32
bf16 = jnp.bfloat16
MESH = pl.DeviceIdType.MESH


def mm(a, b):
    return jnp.dot(a, b, preferred_element_type=f32)


def mm_nt(a, b):
    return lax.dot_general(a, b, (((1,), (1,)), ((), ())), preferred_element_type=f32)


def mm_tn(a, b):
    return lax.dot_general(a, b, (((0,), (0,)), ((), ())), preferred_element_type=f32)


def layer_norm(values, norm_gain):
    average = jnp.mean(values, axis=-1, keepdims=True)
    centred = values - average
    variance = jnp.mean(centred * centred, axis=-1, keepdims=True)
    return centred * lax.rsqrt(variance + norm_eps) * norm_gain


def lanes(shape):
    return lax.broadcasted_iota(jnp.int32, shape, len(shape) - 1)


def noisy_rows(positions, noise_draw, level_hat, level):
    kick = jnp.sqrt(level_hat * level_hat - level * level)
    return [positions[k] + kick * noise_draw[k] for k in range(positions.shape[0])]


def kernel(
    n_row, n_smp,
    positions, noise_draw, noise_level, atom_single, token_single, pair_cond,
    atom_to_token, window_offsets, atom_mask, token_mask, coord_in, atom_gain, atom_qkv,
    atom_proj, gather_in, noise_embed, pair_gain, pair_heads, token_gain, token_qkv,
    token_proj, ffn_in, ffn_out, scatter_out, out_gain, coord_out,
    token_out, direction,
    pair_v, qkv_v, proj_v, fin_v, fout_v,
    spread_heads, bias_all, next_all, q_atom, kv_atom, halo_n, halo_o, mixed_atom, state,
    tokens_all, k_all, v_all, q_tok, mixed_tok, token_state, mask_rows,
    w_sem, pair_sem, halo_send, halo_recv, tok_right, tok_left, tok_recv,
    bias_sx, bias_sib, bias_recv,
):
    row = lax.axis_index("row")
    smp = lax.axis_index("smp")
    cores = 2 if n_smp % 2 == 0 else 1
    n_x = n_smp // cores
    my_x, my_c = smp // cores, smp % cores
    atom_rows, ca = atom_single.shape
    tok_rows, d_model = token_single.shape
    ff = fout_v.shape[0]
    key_count = tok_rows * n_row
    j_keys = pair_cond.shape[1]
    half_rows = tok_rows // HALVES
    head_size = d_model // HEADS
    mask_tiles = atom_rows // 128

    loads = [
        pltpu.make_async_copy(token_qkv, qkv_v, w_sem.at[0]),
        pltpu.make_async_copy(token_proj, proj_v, w_sem.at[1]),
        pltpu.make_async_copy(ffn_in, fin_v, w_sem.at[2]),
        pltpu.make_async_copy(ffn_out, fout_v, w_sem.at[3]),
    ]
    pair_loads = [
        pltpu.make_async_copy(
            pair_cond.at[pl.ds(half * half_rows, half_rows)],
            pair_v.at[pl.ds(half * half_rows, half_rows)],
            pair_sem.at[half],
        )
        for half in range(HALVES)
    ]
    pair_loads[0].start()
    pair_loads[1].start()
    for load in loads:
        load.start()

    barrier = pltpu.get_barrier_semaphore()
    smp_peers = [((my_x + d) % n_x) * cores + my_c for d in range(1, n_x)]
    if cores == 2:
        smp_peers.append(my_x * cores + (1 - my_c))
    for peer in smp_peers:
        pl.semaphore_signal(barrier, inc=1, device_id={"smp": peer}, device_id_type=MESH)

    @pl.when(row > 0)
    def _():
        pl.semaphore_signal(barrier, inc=1, device_id={"row": row - 1}, device_id_type=MESH)

    @pl.when(row < n_row - 1)
    def _():
        pl.semaphore_signal(barrier, inc=1, device_id={"row": row + 1}, device_id_type=MESH)

    has_left = (row + n_row - 1) // n_row
    has_right = (2 * n_row - 2 - row) // n_row


    def halo_copies(phase):
        right = pltpu.make_async_remote_copy(
            src_ref=next_all.at[phase, pl.ds(atom_rows - HALO, HALO)],
            dst_ref=halo_n.at[phase, 0],
            send_sem=halo_send.at[phase, 0],
            recv_sem=halo_recv.at[phase, 0],
            device_id={"row": row + 1},
            device_id_type=MESH,
        )
        left = pltpu.make_async_remote_copy(
            src_ref=next_all.at[phase, pl.ds(0, HALO)],
            dst_ref=halo_n.at[phase, 1],
            send_sem=halo_send.at[phase, 1],
            recv_sem=halo_recv.at[phase, 1],
            device_id={"row": row - 1},
            device_id_type=MESH,
        )
        return right, left

    def halo_start(phase):
        right, left = halo_copies(phase)

        @pl.when(row < n_row - 1)
        def _():
            right.start()

        @pl.when(row > 0)
        def _():
            left.start()

    def halo_finish(phase, w_kv):
        right, left = halo_copies(phase)
        for side, here, copy, base in (
            (0, row > 0, right, 0),
            (1, row < n_row - 1, left, HALO + atom_rows),
        ):

            @pl.when(here)
            def _():
                copy.wait_recv()
                kv_atom[pl.ds(base, HALO), : 2 * ca] = mm(halo_n[phase, side], w_kv).astype(bf16)

            @pl.when(jnp.logical_not(here))
            def _():
                kv_atom[pl.ds(base, HALO), : 2 * ca] = jnp.zeros((HALO, 2 * ca), bf16)

        @pl.when(row < n_row - 1)
        def _():
            right.wait_send()

        @pl.when(row > 0)
        def _():
            left.wait_send()

    level = noise_level[...]
    level_hat = (1.0 + gamma_boost) * level
    noisy = jnp.concatenate(noisy_rows(positions, noise_draw, level_hat, level), axis=0)
    scaled = noisy / jnp.sqrt(level_hat * level_hat + sigma_data * sigma_data)
    state[...] = atom_single[...].astype(f32) + lax.dot_general(
        scaled, coord_in[...], (((0,), (0,)), ((), ())),
        precision=lax.Precision.HIGHEST, preferred_element_type=f32,
    )

    def mask_row(tile):
        top = n_row * mask_tiles
        inside = jnp.logical_and(tile >= 0, tile < top)
        safe = jnp.clip(tile, 0, top - 1)
        values = atom_mask[pl.ds(safe, 1), :].astype(f32)
        return jnp.where(inside, values, jnp.zeros_like(values))

    def build_masks(pair, carry):
        tile = row * mask_tiles + pair
        wide = jnp.concatenate(
            [mask_row(tile - 1), mask_row(tile), mask_row(tile + 1), jnp.zeros((1, 128), f32)], axis=1
        )
        wide = jnp.broadcast_to(wide, (8, 512))
        for odd in range(2):
            start = 32 + 64 * odd
            moved = pltpu.roll(wide, 512 - start, 1)
            mask_rows[2 * pair + odd] = moved[:, :256]
        return carry

    lax.fori_loop(0, mask_tiles, build_masks, 0)

    def normalise_and_send(phase):
        next_all[phase] = layer_norm(state[...], atom_gain[pl.ds(phase, 1), :]).astype(bf16)

    kv_atom[:, 2 * ca :] = jnp.ones((atom_rows + 2 * HALO, ca), bf16)
    normalise_and_send(0)
    pl.semaphore_wait(barrier, len(smp_peers) + has_left + has_right)
    halo_start(0)

    unit = 8
    for i in range(unit):
        pick = lanes((HEADS, 128)) == (
            lax.broadcasted_iota(jnp.int32, (HEADS, 128), 0) * unit + i
        )
        spread_heads[pl.ds(i * 128, 128), :] = mm_tn(
            pair_heads[...], pick.astype(f32).astype(bf16)
        ).astype(bf16)
    mean_matrix = jnp.full((ca, ca), 1.0 / ca, bf16)

    def bias_half(half):
        pair_loads[half].wait()

        def body(step, carry):
            base = half * half_rows + step * 16
            x = pair_v[pl.ds(base, 2 * unit)].reshape(2 * unit * j_keys, ca)
            centred = x.astype(f32) - mm(x, mean_matrix)
            variance = mm((centred * centred).astype(bf16), mean_matrix)
            normed = (centred * lax.rsqrt(variance + norm_eps) * pair_gain[...]).astype(bf16)
            normed = normed.reshape(2 * unit, j_keys, ca)
            parts = []
            for sub in range(2):
                wide = jnp.concatenate([normed[sub * unit + i] for i in range(unit)], axis=1)
                total = mm(wide, spread_heads[...])
                parts.append(jnp.transpose(total).reshape(HEADS, unit, j_keys))
            both = jnp.concatenate(parts, axis=1).astype(bf16)
            bias_all[smp, half, :, pl.ds(pl.multiple_of(step * 16, 16), 16), :] = both
            return carry

        lax.fori_loop(0, half_rows // 16, body, 0)

    def bias_x(half, d):
        return pltpu.make_async_remote_copy(
            src_ref=bias_all.at[smp, half],
            dst_ref=bias_all.at[smp, half],
            send_sem=bias_sx.at[half, d],
            recv_sem=bias_recv.at[half, smp],
            device_id={"smp": ((my_x + d) % n_x) * cores + my_c},
            device_id_type=MESH,
        )

    def bias_to_sibling(half, d):
        slot = ((my_x + n_x - d) % n_x) * cores + my_c
        return pltpu.make_async_remote_copy(
            src_ref=bias_all.at[slot, half],
            dst_ref=bias_all.at[slot, half],
            send_sem=bias_sib.at[half, d],
            recv_sem=bias_recv.at[half, slot],
            device_id={"smp": my_x * cores + (1 - my_c)},
            device_id_type=MESH,
        )

    def bias_arrival(half, d, core):
        slot = ((my_x + n_x - d) % n_x) * cores + core
        return pltpu.make_async_remote_copy(
            src_ref=bias_all.at[slot, half],
            dst_ref=bias_all.at[slot, half],
            send_sem=bias_sx.at[half, 0],
            recv_sem=bias_recv.at[half, slot],
            device_id={"smp": my_x * cores + (1 - my_c) if cores == 2 else smp},
            device_id_type=MESH,
        )

    def bias_send(half):
        for d in range(1, n_x):
            bias_x(half, d).start()
        if cores == 2:
            bias_to_sibling(half, 0).start()

    def bias_relay(half):
        for d in range(1, n_x):
            bias_arrival(half, d, my_c).wait_recv()
            if cores == 2:
                bias_to_sibling(half, d).start()

    def bias_finish(half):
        for d in range(n_x):
            if cores == 2:
                bias_arrival(half, d, 1 - my_c).wait_recv()
                bias_to_sibling(half, d).wait_send()
            if d:
                bias_x(half, d).wait_send()

    head_of_lane = lanes((GQ, ca)) // (ca // AHEADS)
    atom_scale = 1.0 / float(ca // AHEADS) ** 0.5
    group_count = atom_rows // GQ

    def attend_group(group):
        start = pl.multiple_of(group * GQ, GQ)
        queries = q_atom[pl.ds(start, GQ), :]
        zero = jnp.zeros_like(queries)
        stacked = jnp.concatenate(
            [jnp.where(head_of_lane == h, queries, zero) for h in range(AHEADS)], axis=0
        )
        keys = kv_atom[pl.ds(start, 256), :ca]
        values = kv_atom[pl.ds(start, 256), ca:]
        scores = mm_nt(stacked, keys) * atom_scale
        dead = jnp.where(mask_rows[group] > 0, 0.0, masked_score)
        relative = lanes((8, 256))
        rows = []
        for u in range(GQ // WQ):
            first = window_offsets[group * (GQ // WQ) + u] + (HALO + WQ * u)
            inside = (relative >= first) & (relative < first + WK)
            own = jnp.where(inside, dead, outside_score)
            rows += [own] * (WQ // 8)
        limits = jnp.concatenate(rows, axis=0)
        scores = scores.reshape(AHEADS, GQ, 256) + limits[None]
        scores = scores.reshape(AHEADS * GQ, 256)
        largest = jnp.max(scores, axis=-1, keepdims=True)
        exponent = jnp.exp(scores - largest)
        summed = mm(exponent.astype(bf16), values)
        mixed = summed[:, :ca] / summed[:, ca:]
        result = jnp.zeros((GQ, ca), f32)
        for h in range(AHEADS):
            result = jnp.where(head_of_lane == h, mixed[h * GQ : (h + 1) * GQ], result)
        mixed_atom[pl.ds(start, GQ), :] = result.astype(bf16)

    def atom_block(phase, between):
        w_qkv = atom_qkv[phase]
        projected = mm(next_all[phase], w_qkv).astype(bf16)
        q_atom[...] = projected[:, :ca]
        kv_atom[pl.ds(HALO, atom_rows), : 2 * ca] = projected[:, ca:]
        between()

        def body(group, carry):
            attend_group(group)
            return carry

        lax.fori_loop(2, group_count - 2, body, 0, unroll=4)
        halo_finish(phase, w_qkv[:, ca:])

        def edge(k, carry):
            attend_group(k + (k // 2) * (group_count - 4))
            return carry

        lax.fori_loop(0, 4, edge, 0, unroll=4)
        state[...] = state[...] + mm(mixed_atom[...], atom_proj[phase])

    def first_half():
        bias_half(0)
        bias_send(0)

    atom_block(0, first_half)

    ids = atom_to_token[...] - row * tok_rows
    valid = jnp.concatenate([mask_row(row * mask_tiles + k) for k in range(mask_tiles)], axis=1)
    member = (lax.broadcasted_iota(jnp.int32, (tok_rows, atom_rows), 0) == ids) & (valid > 0)
    onehot32 = member.astype(f32)
    onehot = onehot32.astype(bf16)
    counts = jnp.maximum(jnp.sum(onehot32, axis=1, keepdims=True), 1.0)
    lifted = jnp.maximum(mm(state[...].astype(bf16), gather_in[...]), 0.0).astype(bf16)
    embed = jnp.concatenate([noise_embed[k : k + 1, :] for k in range(d_model // 128)], axis=1)
    token_state[...] = (
        mm(onehot, lifted) / counts
        + token_single[...].astype(f32)
        + jnp.log(level_hat / sigma_data) / 4.0 * embed
    )
    tokens_all[row] = layer_norm(token_state[...], token_gain[0:1, :]).astype(bf16)

    def token_copy(slot, sem, target):
        return pltpu.make_async_remote_copy(
            src_ref=tokens_all.at[slot],
            dst_ref=tokens_all.at[slot],
            send_sem=sem.at[slot],
            recv_sem=tok_recv.at[slot],
            device_id={"row": target},
            device_id_type=MESH,
        )

    @pl.when(row < n_row - 1)
    def _():
        token_copy(row, tok_right, row + 1).start()

    @pl.when(row > 0)
    def _():
        token_copy(row, tok_left, row - 1).start()

    bias_half(1)
    bias_send(1)
    bias_relay(0)

    def project_keys(slot):
        x = tokens_all[slot]
        base = pl.multiple_of(slot * tok_rows, tok_rows)
        k_all[pl.ds(base, tok_rows), :] = mm(x, qkv_v[:, d_model : 2 * d_model]).astype(bf16)
        v_all[pl.ds(base, tok_rows), :] = mm(x, qkv_v[:, 2 * d_model :]).astype(bf16)

    loads[0].wait()
    q_tok[...] = mm(tokens_all[row], qkv_v[:, :d_model]).astype(bf16)
    project_keys(row)
    for t in range(1, n_row):

        @pl.when(row >= t)
        def _():
            slot = row - t
            token_copy(slot, tok_left, row - 1).wait_recv()

            @pl.when(row < n_row - 1)
            def _():
                token_copy(slot, tok_right, row + 1).start()

        @pl.when(row + t < n_row)
        def _():
            slot = row + t
            token_copy(slot, tok_right, row + 1).wait_recv()

            @pl.when(row > 0)
            def _():
                token_copy(slot, tok_left, row - 1).start()

        if t == n_row // 2:
            bias_relay(1)

        @pl.when(row >= t)
        def _():
            project_keys(row - t)

        @pl.when(row + t < n_row)
        def _():
            project_keys(row + t)

    bias_finish(0)
    bias_finish(1)

    mixed_tok[...] = jnp.zeros_like(mixed_tok)
    dead_keys = jnp.where(token_mask[...] > 0, 0.0, masked_score)
    token_scale = 1.0 / float(head_size) ** 0.5
    for h in range(HEADS):
        low = min(h * head_size // 128, d_model // 128 - 2) * 128
        window = lanes((tok_rows, 256)) + low
        mine = (window >= h * head_size) & (window < (h + 1) * head_size)
        queries = q_tok[:, low : low + 256]
        queries = jnp.where(mine, queries, jnp.zeros_like(queries))
        bias = jnp.concatenate(
            [bias_all[s, :, h].reshape(tok_rows, j_keys).astype(f32) for s in range(n_smp)], axis=1
        )
        scores = mm_nt(queries, k_all[:, low : low + 256]) * token_scale + bias + dead_keys
        largest = jnp.max(scores, axis=-1, keepdims=True)
        exponent = jnp.exp(scores - largest)
        total = jnp.sum(exponent, axis=-1, keepdims=True)
        mixed = mm(exponent.astype(bf16), v_all[:, low : low + 256]) / total
        mixed_tok[:, low : low + 256] = jnp.where(mine, mixed, mixed_tok[:, low : low + 256])

    loads[1].wait()
    token_state[...] = token_state[...] + mm(mixed_tok[...].astype(bf16), proj_v[...])
    normed = layer_norm(token_state[...], token_gain[1:2, :]).astype(bf16)
    loads[2].wait()
    gate = mm(normed, fin_v[:, :ff])
    active = (gate / (1.0 + jnp.exp(-gate)) * mm(normed, fin_v[:, ff:])).astype(bf16)
    loads[3].wait()
    result = (token_state[...] + mm(active, fout_v[...])).astype(bf16)
    token_out[...] = result
    spread_back = mm(result, scatter_out[...]).astype(bf16)
    state[...] = state[...] + mm_tn(onehot, spread_back)

    normalise_and_send(1)
    halo_start(1)
    atom_block(1, lambda: None)

    normed_out = layer_norm(state[...], out_gain[...]).astype(bf16)
    update = mm_nt(coord_out[...], normed_out)
    for k in range(coord_out.shape[0]):
        direction[k] = update[k : k + 1]

    for slot in range(n_row):

        @pl.when(jnp.logical_and(row < n_row - 1, slot <= row))
        def _():
            token_copy(slot, tok_right, row + 1).wait_send()

        @pl.when(jnp.logical_and(row > 0, slot >= row))
        def _():
            token_copy(slot, tok_left, row - 1).wait_send()


def finish(positions, noise_draw, noise_level, result, update, token_out, direction):
    token_out[...] = result[...]
    level = noise_level[...]
    level_hat = (1.0 + gamma_boost) * level
    base_square = sigma_data * sigma_data + level_hat * level_hat
    skip_scale = sigma_data * sigma_data / base_square
    out_scale = level_hat * sigma_data / jnp.sqrt(base_square)
    for k, noisy in enumerate(noisy_rows(positions, noise_draw, level_hat, level)):
        denoised = skip_scale * noisy + out_scale * update[k]
        direction[k] = (noisy - denoised) / level_hat


def per_device(n_row, n_smp, *args):
    (
        positions, noise_draw, noise_level, atom_single, token_single, pair_cond,
        atom_to_token, window_offsets, atom_mask, token_mask, coord_in, atom_gain, atom_qkv,
        atom_proj, gather_in, noise_embed, pair_gain, pair_heads, token_gain, token_qkv,
        token_proj, ffn_in, ffn_out, scatter_out, out_gain, coord_out,
    ) = args
    atom_rows, ca = atom_single.shape
    tok_rows, d_model = token_single.shape
    j_keys = pair_cond.shape[1]
    key_count = tok_rows * n_row
    vmem = pl.BlockSpec(memory_space=pltpu.VMEM)
    smem = pl.BlockSpec(memory_space=pltpu.SMEM)
    hbm = pl.BlockSpec(memory_space=pl.ANY)
    operands = (
        positions.transpose(1, 0, 2), noise_draw.transpose(1, 0, 2), noise_level.reshape(1, 1), atom_single, token_single,
        pair_cond, atom_to_token.reshape(1, -1), window_offsets, atom_mask.reshape(-1, 128),
        token_mask.reshape(1, -1), coord_in, atom_gain, atom_qkv, atom_proj, gather_in,
        noise_embed.reshape(-1, 128), pair_gain.reshape(1, -1), pair_heads.T, token_gain, token_qkv,
        token_proj, ffn_in, ffn_out, scatter_out, out_gain.reshape(1, -1), coord_out,
    )
    specs = [vmem] * len(operands)
    specs[5] = hbm
    specs[7] = smem
    for i in (19, 20, 21, 22):
        specs[i] = hbm
    dma = pltpu.SemaphoreType.DMA
    shapes = (
        jax.ShapeDtypeStruct((tok_rows, d_model), bf16),
        jax.ShapeDtypeStruct(operands[0].shape, f32),
    )
    result, update = pl.pallas_call(
        functools.partial(kernel, n_row, n_smp),
        out_shape=shapes,
        in_specs=specs,
        out_specs=(vmem, vmem),
        scratch_shapes=[
            pltpu.VMEM(pair_cond.shape, bf16),
            pltpu.VMEM(token_qkv.shape, bf16),
            pltpu.VMEM(token_proj.shape, bf16),
            pltpu.VMEM(ffn_in.shape, bf16),
            pltpu.VMEM(ffn_out.shape, bf16),
            pltpu.VMEM((8 * 128, 128), bf16),
            pltpu.VMEM((n_smp, HALVES, HEADS, tok_rows // HALVES, j_keys), bf16),
            pltpu.VMEM((2, atom_rows, ca), bf16),
            pltpu.VMEM((atom_rows, ca), bf16),
            pltpu.VMEM((atom_rows + 2 * HALO, 3 * ca), bf16),
            pltpu.VMEM((2, 2, HALO, ca), bf16),
            pltpu.VMEM((8, 128), bf16),
            pltpu.VMEM((atom_rows, ca), bf16),
            pltpu.VMEM((atom_rows, ca), f32),
            pltpu.VMEM((n_row, tok_rows, d_model), bf16),
            pltpu.VMEM((key_count, d_model), bf16),
            pltpu.VMEM((key_count, d_model), bf16),
            pltpu.VMEM((tok_rows, d_model), bf16),
            pltpu.VMEM((tok_rows, d_model), f32),
            pltpu.VMEM((tok_rows, d_model), f32),
            pltpu.VMEM((atom_rows // GQ, 8, 256), f32),
            dma((4,)),
            dma((HALVES,)),
            dma((2, 2)),
            dma((2, 2)),
            dma((n_row,)),
            dma((n_row,)),
            dma((n_row,)),
            dma((HALVES, n_smp)),
            dma((HALVES, n_smp)),
            dma((HALVES, n_smp)),
        ],
        compiler_params=pltpu.CompilerParams(
            collective_id=0, has_side_effects=True, vmem_limit_bytes=60 * 1024 * 1024
        ),
    )(*operands)
    token_out, direction = pl.pallas_call(
        finish, out_shape=shapes, in_specs=[vmem] * 5, out_specs=(vmem, vmem)
    )(*operands[:3], result, update)
    return token_out[None], direction.transpose(1, 0, 2)


def solution(mesh):
    in_specs = (
        P(("grp", "smp"), None, "row"),
        P(("grp", "smp"), None, "row"),
        P(("grp", "smp")),
        P(("grp", "row"), None),
        P(("grp", "row"), None),
        P(("grp", "row"), "smp", None),
        P(("grp", "row")),
        P(("grp", "row")),
        P("grp"),
        P("grp"),
    ) + (P(),) * 16
    out_specs = (P(("grp", "smp"), "row", None), P(("grp", "smp"), None, "row"))
    return jax.shard_map(
        functools.partial(per_device, mesh.shape["row"], mesh.shape["smp"]),
        mesh=mesh, in_specs=in_specs, out_specs=out_specs, check_vma=False,
    )
```

```python
import functools
import jax
import jax.numpy as jnp
from jax import lax
from jax.experimental import pallas as pl
from jax.experimental.pallas import tpu as pltpu
from jax.sharding import PartitionSpec as P

HEADS = 16
AHEADS = 4
WQ = 32
WK = 128
HALO = 96
GQ = 64
HALVES = 4

sigma_data = 16.0
gamma_boost = 0.8
norm_eps = 1e-05
masked_score = -1e30
outside_score = -2e30

f32 = jnp.float32
bf16 = jnp.bfloat16
MESH = pl.DeviceIdType.MESH


def mm(a, b):
    return jnp.dot(a, b, preferred_element_type=f32)


def mm_nt(a, b):
    return lax.dot_general(a, b, (((1,), (1,)), ((), ())), preferred_element_type=f32)


def mm_tn(a, b):
    return lax.dot_general(a, b, (((0,), (0,)), ((), ())), preferred_element_type=f32)


def layer_norm(values, norm_gain):
    average = jnp.mean(values, axis=-1, keepdims=True)
    centred = values - average
    variance = jnp.mean(centred * centred, axis=-1, keepdims=True)
    return centred * lax.rsqrt(variance + norm_eps) * norm_gain


def lanes(shape):
    return lax.broadcasted_iota(jnp.int32, shape, len(shape) - 1)


def noisy_rows(positions, noise_draw, level_hat, level):
    kick = jnp.sqrt(level_hat * level_hat - level * level)
    return [positions[k] + kick * noise_draw[k] for k in range(positions.shape[0])]


def kernel(
    n_row, n_smp,
    positions, noise_draw, noise_level, atom_single, token_single, pair_cond,
    atom_to_token, window_offsets, atom_mask, token_mask, coord_in, atom_gain, atom_qkv,
    atom_proj, gather_in, noise_embed, pair_gain, pair_heads, token_gain, token_qkv,
    token_proj, ffn_in, ffn_out, scatter_out, out_gain, coord_out,
    token_out, direction,
    pair_v, qkv_v, proj_v, fin_v, fout_v,
    spread_heads, bias_all, next_all, q_atom, kv_atom, halo_n, halo_o, mixed_atom, state,
    tokens_all, k_all, v_all, q_tok, mixed_tok, token_state, mask_rows,
    w_sem, pair_sem, halo_send, halo_recv, tok_right, tok_left, tok_recv,
    bias_sx, bias_sib, bias_recv,
):
    row = lax.axis_index("row")
    smp = lax.axis_index("smp")
    cores = 2 if n_smp % 2 == 0 else 1
    n_x = n_smp // cores
    my_x, my_c = smp // cores, smp % cores
    atom_rows, ca = atom_single.shape
    tok_rows, d_model = token_single.shape
    ff = fout_v.shape[0]
    key_count = tok_rows * n_row
    j_keys = pair_cond.shape[1]
    half_rows = tok_rows // HALVES
    head_size = d_model // HEADS
    mask_tiles = atom_rows // 128

    loads = [
        pltpu.make_async_copy(token_qkv, qkv_v, w_sem.at[0]),
        pltpu.make_async_copy(token_proj, proj_v, w_sem.at[1]),
        pltpu.make_async_copy(ffn_in, fin_v, w_sem.at[2]),
        pltpu.make_async_copy(ffn_out, fout_v, w_sem.at[3]),
    ]
    pair_loads = [
        pltpu.make_async_copy(
            pair_cond.at[pl.ds(half * half_rows, half_rows)],
            pair_v.at[pl.ds(half * half_rows, half_rows)],
            pair_sem.at[half],
        )
        for half in range(HALVES)
    ]
    for load in pair_loads:
        load.start()
    for load in loads:
        load.start()

    barrier = pltpu.get_barrier_semaphore()
    smp_peers = [((my_x + d) % n_x) * cores + my_c for d in range(1, n_x)]
    if cores == 2:
        smp_peers.append(my_x * cores + (1 - my_c))
    for peer in smp_peers:
        pl.semaphore_signal(barrier, inc=1, device_id={"smp": peer}, device_id_type=MESH)

    @pl.when(row > 0)
    def _():
        pl.semaphore_signal(barrier, inc=1, device_id={"row": row - 1}, device_id_type=MESH)

    @pl.when(row < n_row - 1)
    def _():
        pl.semaphore_signal(barrier, inc=1, device_id={"row": row + 1}, device_id_type=MESH)

    has_left = (row + n_row - 1) // n_row
    has_right = (2 * n_row - 2 - row) // n_row


    def halo_copies(phase):
        right = pltpu.make_async_remote_copy(
            src_ref=next_all.at[phase, pl.ds(atom_rows - HALO, HALO)],
            dst_ref=halo_n.at[phase, 0],
            send_sem=halo_send.at[phase, 0],
            recv_sem=halo_recv.at[phase, 0],
            device_id={"row": row + 1},
            device_id_type=MESH,
        )
        left = pltpu.make_async_remote_copy(
            src_ref=next_all.at[phase, pl.ds(0, HALO)],
            dst_ref=halo_n.at[phase, 1],
            send_sem=halo_send.at[phase, 1],
            recv_sem=halo_recv.at[phase, 1],
            device_id={"row": row - 1},
            device_id_type=MESH,
        )
        return right, left

    def halo_start(phase):
        right, left = halo_copies(phase)

        @pl.when(row < n_row - 1)
        def _():
            right.start()

        @pl.when(row > 0)
        def _():
            left.start()

    def halo_finish(phase, w_kv):
        right, left = halo_copies(phase)
        for side, here, copy, base in (
            (0, row > 0, right, 0),
            (1, row < n_row - 1, left, HALO + atom_rows),
        ):

            @pl.when(here)
            def _():
                copy.wait_recv()
                kv_atom[pl.ds(base, HALO), : 2 * ca] = mm(halo_n[phase, side], w_kv).astype(bf16)

            @pl.when(jnp.logical_not(here))
            def _():
                kv_atom[pl.ds(base, HALO), : 2 * ca] = jnp.zeros((HALO, 2 * ca), bf16)

        @pl.when(row < n_row - 1)
        def _():
            right.wait_send()

        @pl.when(row > 0)
        def _():
            left.wait_send()

    level = noise_level[...]
    level_hat = (1.0 + gamma_boost) * level
    noisy = jnp.concatenate(noisy_rows(positions, noise_draw, level_hat, level), axis=0)
    scaled = noisy / jnp.sqrt(level_hat * level_hat + sigma_data * sigma_data)
    state[...] = atom_single[...].astype(f32) + lax.dot_general(
        scaled, coord_in[...], (((0,), (0,)), ((), ())),
        precision=lax.Precision.HIGHEST, preferred_element_type=f32,
    )

    def mask_row(tile):
        top = n_row * mask_tiles
        inside = jnp.logical_and(tile >= 0, tile < top)
        safe = jnp.clip(tile, 0, top - 1)
        values = atom_mask[pl.ds(safe, 1), :].astype(f32)
        return jnp.where(inside, values, jnp.zeros_like(values))

    def build_masks(pair, carry):
        tile = row * mask_tiles + pair
        wide = jnp.concatenate(
            [mask_row(tile - 1), mask_row(tile), mask_row(tile + 1), jnp.zeros((1, 128), f32)], axis=1
        )
        wide = jnp.broadcast_to(wide, (8, 512))
        for odd in range(2):
            start = 32 + 64 * odd
            moved = pltpu.roll(wide, 512 - start, 1)
            mask_rows[2 * pair + odd] = moved[:, :256]
        return carry

    lax.fori_loop(0, mask_tiles, build_masks, 0)

    def normalise_and_send(phase):
        next_all[phase] = layer_norm(state[...], atom_gain[pl.ds(phase, 1), :]).astype(bf16)

    kv_atom[:, 2 * ca :] = jnp.ones((atom_rows + 2 * HALO, ca), bf16)
    normalise_and_send(0)
    pl.semaphore_wait(barrier, len(smp_peers) + has_left + has_right)
    halo_start(0)

    unit = 8
    for i in range(unit):
        pick = lanes((HEADS, 128)) == (
            lax.broadcasted_iota(jnp.int32, (HEADS, 128), 0) * unit + i
        )
        spread_heads[pl.ds(i * 128, 128), :] = mm_tn(
            pair_heads[...], pick.astype(f32).astype(bf16)
        ).astype(bf16)
    mean_matrix = jnp.full((ca, ca), 1.0 / ca, bf16)

    def bias_half(half):
        pair_loads[half].wait()

        def body(step, carry):
            base = half * half_rows + step * 16
            x = pair_v[pl.ds(base, 2 * unit)].reshape(2 * unit * j_keys, ca)
            centred = x.astype(f32) - mm(x, mean_matrix)
            variance = mm((centred * centred).astype(bf16), mean_matrix)
            normed = (centred * lax.rsqrt(variance + norm_eps) * pair_gain[...]).astype(bf16)
            normed = normed.reshape(2 * unit, j_keys, ca)
            parts = []
            for sub in range(2):
                wide = jnp.concatenate([normed[sub * unit + i] for i in range(unit)], axis=1)
                total = mm(wide, spread_heads[...])
                parts.append(jnp.transpose(total).reshape(HEADS, unit, j_keys))
            both = jnp.concatenate(parts, axis=1).astype(bf16)
            bias_all[smp, half, :, pl.ds(pl.multiple_of(step * 16, 16), 16), :] = both
            return carry

        lax.fori_loop(0, half_rows // 16, body, 0)

    def bias_x(half, d):
        return pltpu.make_async_remote_copy(
            src_ref=bias_all.at[smp, half],
            dst_ref=bias_all.at[smp, half],
            send_sem=bias_sx.at[half, d],
            recv_sem=bias_recv.at[half, smp],
            device_id={"smp": ((my_x + d) % n_x) * cores + my_c},
            device_id_type=MESH,
        )

    def bias_to_sibling(half, d):
        slot = ((my_x + n_x - d) % n_x) * cores + my_c
        return pltpu.make_async_remote_copy(
            src_ref=bias_all.at[slot, half],
            dst_ref=bias_all.at[slot, half],
            send_sem=bias_sib.at[half, d],
            recv_sem=bias_recv.at[half, slot],
            device_id={"smp": my_x * cores + (1 - my_c)},
            device_id_type=MESH,
        )

    def bias_arrival(half, d, core):
        slot = ((my_x + n_x - d) % n_x) * cores + core
        return pltpu.make_async_remote_copy(
            src_ref=bias_all.at[slot, half],
            dst_ref=bias_all.at[slot, half],
            send_sem=bias_sx.at[half, 0],
            recv_sem=bias_recv.at[half, slot],
            device_id={"smp": my_x * cores + (1 - my_c) if cores == 2 else smp},
            device_id_type=MESH,
        )

    def bias_send(half):
        for d in range(1, n_x):
            bias_x(half, d).start()
        if cores == 2:
            bias_to_sibling(half, 0).start()

    def bias_relay(half):
        for d in range(1, n_x):
            bias_arrival(half, d, my_c).wait_recv()
            if cores == 2:
                bias_to_sibling(half, d).start()

    def bias_finish(half):
        for d in range(n_x):
            if cores == 2:
                bias_arrival(half, d, 1 - my_c).wait_recv()
                bias_to_sibling(half, d).wait_send()
            if d:
                bias_x(half, d).wait_send()

    head_of_lane = lanes((GQ, ca)) // (ca // AHEADS)
    atom_scale = 1.0 / float(ca // AHEADS) ** 0.5
    group_count = atom_rows // GQ

    def attend_group(group):
        start = pl.multiple_of(group * GQ, GQ)
        queries = q_atom[pl.ds(start, GQ), :]
        zero = jnp.zeros_like(queries)
        stacked = jnp.concatenate(
            [jnp.where(head_of_lane == h, queries, zero) for h in range(AHEADS)], axis=0
        )
        keys = kv_atom[pl.ds(start, 256), :ca]
        values = kv_atom[pl.ds(start, 256), ca:]
        scores = mm_nt(stacked, keys) * atom_scale
        dead = jnp.where(mask_rows[group] > 0, 0.0, masked_score)
        relative = lanes((8, 256))
        rows = []
        for u in range(GQ // WQ):
            first = window_offsets[group * (GQ // WQ) + u] + (HALO + WQ * u)
            inside = (relative >= first) & (relative < first + WK)
            own = jnp.where(inside, dead, outside_score)
            rows += [own] * (WQ // 8)
        limits = jnp.concatenate(rows, axis=0)
        scores = scores.reshape(AHEADS, GQ, 256) + limits[None]
        scores = scores.reshape(AHEADS * GQ, 256)
        largest = jnp.max(scores, axis=-1, keepdims=True)
        exponent = jnp.exp(scores - largest)
        summed = mm(exponent.astype(bf16), values)
        mixed = summed[:, :ca] / summed[:, ca:]
        result = jnp.zeros((GQ, ca), f32)
        for h in range(AHEADS):
            result = jnp.where(head_of_lane == h, mixed[h * GQ : (h + 1) * GQ], result)
        mixed_atom[pl.ds(start, GQ), :] = result.astype(bf16)

    def atom_block(phase, between):
        w_qkv = atom_qkv[phase]
        projected = mm(next_all[phase], w_qkv).astype(bf16)
        q_atom[...] = projected[:, :ca]
        kv_atom[pl.ds(HALO, atom_rows), : 2 * ca] = projected[:, ca:]
        between()

        def body(group, carry):
            attend_group(group)
            return carry

        lax.fori_loop(2, group_count - 2, body, 0, unroll=4)
        halo_finish(phase, w_qkv[:, ca:])

        def edge(k, carry):
            attend_group(k + (k // 2) * (group_count - 4))
            return carry

        lax.fori_loop(0, 4, edge, 0, unroll=4)
        state[...] = state[...] + mm(mixed_atom[...], atom_proj[phase])

    def first_half():
        bias_half(0)
        bias_send(0)

    atom_block(0, first_half)

    ids = atom_to_token[...] - row * tok_rows
    valid = jnp.concatenate([mask_row(row * mask_tiles + k) for k in range(mask_tiles)], axis=1)
    member = (lax.broadcasted_iota(jnp.int32, (tok_rows, atom_rows), 0) == ids) & (valid > 0)
    onehot32 = member.astype(f32)
    onehot = onehot32.astype(bf16)
    counts = jnp.maximum(jnp.sum(onehot32, axis=1, keepdims=True), 1.0)
    lifted = jnp.maximum(mm(state[...].astype(bf16), gather_in[...]), 0.0).astype(bf16)
    embed = jnp.concatenate([noise_embed[k : k + 1, :] for k in range(d_model // 128)], axis=1)
    token_state[...] = (
        mm(onehot, lifted) / counts
        + token_single[...].astype(f32)
        + jnp.log(level_hat / sigma_data) / 4.0 * embed
    )
    tokens_all[row] = layer_norm(token_state[...], token_gain[0:1, :]).astype(bf16)

    def token_copy(slot, sem, target):
        return pltpu.make_async_remote_copy(
            src_ref=tokens_all.at[slot],
            dst_ref=tokens_all.at[slot],
            send_sem=sem.at[slot],
            recv_sem=tok_recv.at[slot],
            device_id={"row": target},
            device_id_type=MESH,
        )

    @pl.when(row < n_row - 1)
    def _():
        token_copy(row, tok_right, row + 1).start()

    @pl.when(row > 0)
    def _():
        token_copy(row, tok_left, row - 1).start()

    for part in range(1, HALVES):
        bias_half(part)
        bias_send(part)
    bias_relay(0)
    relayed = 1

    def project_keys(slot):
        x = tokens_all[slot]
        base = pl.multiple_of(slot * tok_rows, tok_rows)
        k_all[pl.ds(base, tok_rows), :] = mm(x, qkv_v[:, d_model : 2 * d_model]).astype(bf16)
        v_all[pl.ds(base, tok_rows), :] = mm(x, qkv_v[:, 2 * d_model :]).astype(bf16)

    loads[0].wait()
    q_tok[...] = mm(tokens_all[row], qkv_v[:, :d_model]).astype(bf16)
    project_keys(row)
    for t in range(1, n_row):

        @pl.when(row >= t)
        def _():
            slot = row - t
            token_copy(slot, tok_left, row - 1).wait_recv()

            @pl.when(row < n_row - 1)
            def _():
                token_copy(slot, tok_right, row + 1).start()

        @pl.when(row + t < n_row)
        def _():
            slot = row + t
            token_copy(slot, tok_right, row + 1).wait_recv()

            @pl.when(row > 0)
            def _():
                token_copy(slot, tok_left, row - 1).start()

        share = HALVES if t == n_row - 1 else min(HALVES, 1 + t)
        for part in range(relayed, share):
            bias_relay(part)
        relayed = share

        @pl.when(row >= t)
        def _():
            project_keys(row - t)

        @pl.when(row + t < n_row)
        def _():
            project_keys(row + t)

    for part in range(relayed, HALVES):
        bias_relay(part)
    for part in range(HALVES):
        bias_finish(part)

    mixed_tok[...] = jnp.zeros_like(mixed_tok)
    dead_keys = jnp.where(token_mask[...] > 0, 0.0, masked_score)
    token_scale = 1.0 / float(head_size) ** 0.5
    for h in range(HEADS):
        low = min(h * head_size // 128, d_model // 128 - 2) * 128
        window = lanes((tok_rows, 256)) + low
        mine = (window >= h * head_size) & (window < (h + 1) * head_size)
        queries = q_tok[:, low : low + 256]
        queries = jnp.where(mine, queries, jnp.zeros_like(queries))
        bias = jnp.concatenate(
            [bias_all[s, :, h].reshape(tok_rows, j_keys).astype(f32) for s in range(n_smp)], axis=1
        )
        scores = mm_nt(queries, k_all[:, low : low + 256]) * token_scale + bias + dead_keys
        largest = jnp.max(scores, axis=-1, keepdims=True)
        exponent = jnp.exp(scores - largest)
        total = jnp.sum(exponent, axis=-1, keepdims=True)
        mixed = mm(exponent.astype(bf16), v_all[:, low : low + 256]) / total
        mixed_tok[:, low : low + 256] = jnp.where(mine, mixed, mixed_tok[:, low : low + 256])

    loads[1].wait()
    token_state[...] = token_state[...] + mm(mixed_tok[...].astype(bf16), proj_v[...])
    normed = layer_norm(token_state[...], token_gain[1:2, :]).astype(bf16)
    loads[2].wait()
    gate = mm(normed, fin_v[:, :ff])
    active = (gate / (1.0 + jnp.exp(-gate)) * mm(normed, fin_v[:, ff:])).astype(bf16)
    loads[3].wait()
    result = (token_state[...] + mm(active, fout_v[...])).astype(bf16)
    token_out[...] = result
    spread_back = mm(result, scatter_out[...]).astype(bf16)
    state[...] = state[...] + mm_tn(onehot, spread_back)

    normalise_and_send(1)
    halo_start(1)
    atom_block(1, lambda: None)

    normed_out = layer_norm(state[...], out_gain[...]).astype(bf16)
    update = mm_nt(coord_out[...], normed_out)
    for k in range(coord_out.shape[0]):
        direction[k] = update[k : k + 1]

    for slot in range(n_row):

        @pl.when(jnp.logical_and(row < n_row - 1, slot <= row))
        def _():
            token_copy(slot, tok_right, row + 1).wait_send()

        @pl.when(jnp.logical_and(row > 0, slot >= row))
        def _():
            token_copy(slot, tok_left, row - 1).wait_send()


def finish(positions, noise_draw, noise_level, result, update, token_out, direction):
    token_out[...] = result[...]
    level = noise_level[...]
    level_hat = (1.0 + gamma_boost) * level
    base_square = sigma_data * sigma_data + level_hat * level_hat
    skip_scale = sigma_data * sigma_data / base_square
    out_scale = level_hat * sigma_data / jnp.sqrt(base_square)
    for k, noisy in enumerate(noisy_rows(positions, noise_draw, level_hat, level)):
        denoised = skip_scale * noisy + out_scale * update[k]
        direction[k] = (noisy - denoised) / level_hat


def per_device(n_row, n_smp, *args):
    (
        positions, noise_draw, noise_level, atom_single, token_single, pair_cond,
        atom_to_token, window_offsets, atom_mask, token_mask, coord_in, atom_gain, atom_qkv,
        atom_proj, gather_in, noise_embed, pair_gain, pair_heads, token_gain, token_qkv,
        token_proj, ffn_in, ffn_out, scatter_out, out_gain, coord_out,
    ) = args
    atom_rows, ca = atom_single.shape
    tok_rows, d_model = token_single.shape
    j_keys = pair_cond.shape[1]
    key_count = tok_rows * n_row
    vmem = pl.BlockSpec(memory_space=pltpu.VMEM)
    smem = pl.BlockSpec(memory_space=pltpu.SMEM)
    hbm = pl.BlockSpec(memory_space=pl.ANY)
    operands = (
        positions.transpose(1, 0, 2), noise_draw.transpose(1, 0, 2), noise_level.reshape(1, 1), atom_single, token_single,
        pair_cond, atom_to_token.reshape(1, -1), window_offsets, atom_mask.reshape(-1, 128),
        token_mask.reshape(1, -1), coord_in, atom_gain, atom_qkv, atom_proj, gather_in,
        noise_embed.reshape(-1, 128), pair_gain.reshape(1, -1), pair_heads.T, token_gain, token_qkv,
        token_proj, ffn_in, ffn_out, scatter_out, out_gain.reshape(1, -1), coord_out,
    )
    specs = [vmem] * len(operands)
    specs[5] = hbm
    specs[7] = smem
    for i in (19, 20, 21, 22):
        specs[i] = hbm
    dma = pltpu.SemaphoreType.DMA
    shapes = (
        jax.ShapeDtypeStruct((tok_rows, d_model), bf16),
        jax.ShapeDtypeStruct(operands[0].shape, f32),
    )
    result, update = pl.pallas_call(
        functools.partial(kernel, n_row, n_smp),
        out_shape=shapes,
        in_specs=specs,
        out_specs=(vmem, vmem),
        scratch_shapes=[
            pltpu.VMEM(pair_cond.shape, bf16),
            pltpu.VMEM(token_qkv.shape, bf16),
            pltpu.VMEM(token_proj.shape, bf16),
            pltpu.VMEM(ffn_in.shape, bf16),
            pltpu.VMEM(ffn_out.shape, bf16),
            pltpu.VMEM((8 * 128, 128), bf16),
            pltpu.VMEM((n_smp, HALVES, HEADS, tok_rows // HALVES, j_keys), bf16),
            pltpu.VMEM((2, atom_rows, ca), bf16),
            pltpu.VMEM((atom_rows, ca), bf16),
            pltpu.VMEM((atom_rows + 2 * HALO, 3 * ca), bf16),
            pltpu.VMEM((2, 2, HALO, ca), bf16),
            pltpu.VMEM((8, 128), bf16),
            pltpu.VMEM((atom_rows, ca), bf16),
            pltpu.VMEM((atom_rows, ca), f32),
            pltpu.VMEM((n_row, tok_rows, d_model), bf16),
            pltpu.VMEM((key_count, d_model), bf16),
            pltpu.VMEM((key_count, d_model), bf16),
            pltpu.VMEM((tok_rows, d_model), bf16),
            pltpu.VMEM((tok_rows, d_model), f32),
            pltpu.VMEM((tok_rows, d_model), f32),
            pltpu.VMEM((atom_rows // GQ, 8, 256), f32),
            dma((4,)),
            dma((HALVES,)),
            dma((2, 2)),
            dma((2, 2)),
            dma((n_row,)),
            dma((n_row,)),
            dma((n_row,)),
            dma((HALVES, n_smp)),
            dma((HALVES, n_smp)),
            dma((HALVES, n_smp)),
        ],
        compiler_params=pltpu.CompilerParams(
            collective_id=0, has_side_effects=True, vmem_limit_bytes=60 * 1024 * 1024
        ),
    )(*operands)
    token_out, direction = pl.pallas_call(
        finish, out_shape=shapes, in_specs=[vmem] * 5, out_specs=(vmem, vmem)
    )(*operands[:3], result, update)
    return token_out[None], direction.transpose(1, 0, 2)


def solution(mesh):
    in_specs = (
        P(("grp", "smp"), None, "row"),
        P(("grp", "smp"), None, "row"),
        P(("grp", "smp")),
        P(("grp", "row"), None),
        P(("grp", "row"), None),
        P(("grp", "row"), "smp", None),
        P(("grp", "row")),
        P(("grp", "row")),
        P("grp"),
        P("grp"),
    ) + (P(),) * 16
    out_specs = (P(("grp", "smp"), "row", None), P(("grp", "smp"), None, "row"))
    return jax.shard_map(
        functools.partial(per_device, mesh.shape["row"], mesh.shape["smp"]),
        mesh=mesh, in_specs=in_specs, out_specs=out_specs, check_vma=False,
    )
```
